32 devices in a mesh: dp: 16 (over z, y, core), tensor: 2 (over x).
Axes of the slice: x: 2, y: 2, z: 4, core: 2. Of those that a mesh axis runs over, the one named last changes fastest.
Arguments:
- x_in: bfloat16 [37632, 512], P(('dp', 'tensor')), may hold values from -6 to 6
- cot: bfloat16 [37632, 512], P(('dp', 'tensor')), may hold values from -6 to 6
- qkv_weight: bfloat16 [2, 512, 3, 512], P(None, 'dp', None, 'tensor'), may hold values from -0.25 to 0.25
- proj_weight: bfloat16 [2, 512, 512], P(None, 'tensor', 'dp'), may hold values from -0.75 to 0.75
- fc1_weight: bfloat16 [2, 512, 2048], P(None, 'dp', 'tensor'), may hold values from -0.25 to 0.25
- fc2_weight: bfloat16 [2, 2048, 512], P(None, 'tensor', 'dp'), may hold values from -0.125 to 0.125
- layer_norm_gains: float32 [2, 2, 512], replicated, may hold values from 0.5 to 1.5
- layer_norm_biases: float32 [2, 2, 512], replicated, may hold values from -3 to 3
- qv_bias: float32 [2, 2, 512], P(None, None, 'tensor'), may hold values from -3 to 3
- out_bias: float32 [2, 2, 512], replicated, may hold values from -3 to 3
- fc1_bias: float32 [2, 2048], P(None, 'tensor'), may hold values from -3 to 3
- rel_table: float32 [2, 169, 16], P(None, None, 'tensor'), may hold values from -4 to 252, as said below
- rel_index: int32 [49, 49], replicated, may hold values from 0 to 168
- region_ids: int32 [14, 14], replicated, may hold values from 0 to 2
Outputs:
- out: bfloat16 [37632, 512], P(('dp', 'tensor'))
- d_in: float32 [37632, 512], P(('dp', 'tensor'))
- g_qkv_weight: float32 [2, 512, 3, 512], P(None, 'dp', None, 'tensor')
- g_proj_weight: float32 [2, 512, 512], P(None, 'tensor', 'dp')
- g_fc1_weight: float32 [2, 512, 2048], P(None, 'dp', 'tensor')
- g_fc2_weight: float32 [2, 2048, 512], P(None, 'tensor', 'dp')
- g_norm_gain: float32 [2, 2, 512], replicated
- g_norm_shift: float32 [2, 2, 512], replicated
- g_qv_bias: float32 [2, 2, 512], P(None, None, 'tensor')
- g_out_bias: float32 [2, 2, 512], replicated
- g_fc1_bias: float32 [2, 2048], P(None, 'tensor')
- g_rel_table: float32 [2, 169, 16], P(None, None, 'tensor')
The draws below stay inside these ranges and needn't reach their ends.
Inputs may be any that keep to these rules, and one draw needn't show every extreme that they name: `rel_table`: bias of each head for each relative offset. `rel_index`: entry of the table's second dimension for each pair of positions in a window. `region_ids`: in the shifted block two tokens of one window attend to each other only where the ids of their rolled grid cells agree.
All inputs are finite; a program needn't handle non-finite values.
Results may differ from the reference program's by a relative error of at most 0.019.
Values may be sent and summed in bfloat16 or wider, within the bound.
No kernel may reach another device: no remote copies, remote signals or barrier semaphores. Data moves between devices by JAX's collectives and lax.ppermute only.
A program may use at most 320 MiB of HBM per device.

```python
import jax
import jax.numpy as jnp
from jax import lax

D = 512
HEADS = 16
FF = 2048
GRID = 14
WIN = 7
LAYERS = 2
SHIFT = 3
TABLE = 169
TOKENS = 37632
N_DP = 16


def draw_rel_table(key, part):
    base_draw = jnp.clip(jax.random.normal(key, (LAYERS, TABLE, HEADS), jnp.float32), -4.0, 4.0)
    return base_draw


def with_ends(result, rng, smallest, largest):
    longest = result.shape.index(max(result.shape))
    spots = []
    for shift in (0, 1):
        where = [jax.random.randint(jax.random.fold_in(rng, axis), (), 0, length) for axis, length in enumerate(result.shape)]
        where[longest] = (where[longest] + shift) % result.shape[longest]
        spots.append(tuple(where))
    return result.at[spots[0]].set(smallest).at[spots[1]].set(largest)


def level_of(stream_key, dims, pieces, smallest, largest):
    def one(axis_at, blocks):
        heights = jax.random.uniform(jax.random.fold_in(jax.random.fold_in(stream_key, 6), axis_at), (blocks,), jnp.float32, smallest / len(pieces), largest / len(pieces))
        return jnp.repeat(jnp.exp(heights), dims[axis_at] // blocks).reshape((-1,) + (1,) * (len(dims) - axis_at - 1))

    loudness = one(*pieces[0])
    for cut in pieces[1:]:
        loudness = loudness * one(*cut)
    return loudness


def scatter_about(own_key, dims, deviation, limit, pieces=(), held_as=jnp.bfloat16):
    array = deviation * jax.random.normal(own_key, dims, jnp.float32)
    if pieces:
        array = array * level_of(own_key, dims, pieces, -0.22, 0.18)
    return jnp.clip(array, -limit, limit).astype(held_as)


def setup_inputs(seed: int = 0) -> dict:
    streams_of = jax.random.split(jax.random.key(seed), 15)
    return {
        "x_in": scatter_about(streams_of[0], (TOKENS, D), 1.0, 6.0, ((0, 32),)),
        "cot": scatter_about(streams_of[1], (TOKENS, D), 1.0, 6.0, ((0, 32),)),
        "qkv_weight": scatter_about(streams_of[2], (LAYERS, D, 3, D), D ** -0.5, 0.25, ((1, 16), (3, 2))),
        "proj_weight": scatter_about(streams_of[3], (LAYERS, D, D), (D // WIN) ** -0.5, 0.75, ((1, 2), (2, 16))),
        "fc1_weight": scatter_about(streams_of[4], (LAYERS, D, FF), D ** -0.5, 0.25, ((1, 16), (2, 2))),
        "fc2_weight": scatter_about(streams_of[5], (LAYERS, FF, D), FF ** -0.5, 0.125, ((1, 2), (2, 16))),
        "layer_norm_gains": jnp.clip(1.0 + 0.1 * jax.random.normal(streams_of[6], (LAYERS, 2, D), jnp.float32), 0.5, 1.5),
        "layer_norm_biases": scatter_about(streams_of[7], (LAYERS, 2, D), 0.5, 3.0, (), jnp.float32),
        "qv_bias": scatter_about(streams_of[8], (LAYERS, 2, D), 0.5, 3.0, ((2, 2),), jnp.float32),
        "out_bias": scatter_about(streams_of[9], (LAYERS, 2, D), 0.5, 3.0, (), jnp.float32),
        "fc1_bias": scatter_about(streams_of[10], (LAYERS, FF), 0.5, 3.0, ((1, 2),), jnp.float32),
        "rel_table": draw_rel_table(jax.random.fold_in(streams_of[14], 71), 0),
        "rel_index": with_ends(jax.random.randint(streams_of[12], (WIN * WIN, WIN * WIN), 0, TABLE), jax.random.fold_in(streams_of[12], 1), 0, TABLE - 1).astype(jnp.int32),
        "region_ids": with_ends(jax.random.randint(streams_of[13], (GRID, GRID), 0, 3), jax.random.fold_in(streams_of[13], 1), 0, 2).astype(jnp.int32),
    }


epsilon = 1e-05
excluded_score = -1e+30
root_half = 0.7071067811865476
gauss_factor = 0.3989422804014327

def to_bf16(values):
    return lax.optimization_barrier(values.astype(jnp.bfloat16))

def layer_norm_forward(residual_state, gain_vector, bias_vector):
    centered_input = residual_state - lax.optimization_barrier(jnp.mean(residual_state, axis=-1, keepdims=True))
    inverse_deviation = lax.rsqrt(lax.optimization_barrier(jnp.mean(centered_input * centered_input, axis=-1, keepdims=True)) + epsilon)
    standardized_input = centered_input * inverse_deviation
    return (standardized_input * gain_vector + bias_vector, standardized_input, inverse_deviation)

def layer_norm_backward(output_gradient, standardized_input, inverse_deviation, gain_vector):
    scaled_rows = output_gradient * gain_vector
    residual_gradient = inverse_deviation * (scaled_rows - lax.optimization_barrier(jnp.mean(scaled_rows, axis=-1, keepdims=True)) - standardized_input * lax.optimization_barrier(jnp.mean(scaled_rows * standardized_input, axis=-1, keepdims=True)))
    return (residual_gradient, lax.optimization_barrier(jnp.sum(output_gradient * standardized_input, axis=0)), lax.optimization_barrier(jnp.sum(output_gradient, axis=0)))

def gelu_value(preactivation_value):
    return 0.5 * preactivation_value * (1.0 + lax.erf(preactivation_value * root_half))

def gelu_slope(preactivation_value):
    return 0.5 * (1.0 + lax.erf(preactivation_value * root_half)) + preactivation_value * jnp.exp(-0.5 * preactivation_value * preactivation_value) * gauss_factor

def to_windows(rows, shift_offset):
    channels = rows.shape[1]
    images = rows.shape[0] // (GRID * GRID)
    across = GRID // WIN
    image_grid = rows.reshape(images, GRID, GRID, channels)
    if shift_offset:
        image_grid = jnp.roll(image_grid, (-shift_offset, -shift_offset), axis=(1, 2))
    image_grid = image_grid.reshape(images, across, WIN, across, WIN, channels).transpose(0, 1, 3, 2, 4, 5)
    return image_grid.reshape(images * across * across, WIN * WIN, channels)

def from_windows(windowed, shift_offset):
    channels = windowed.shape[2]
    across = GRID // WIN
    images = windowed.shape[0] // (across * across)
    image_grid = windowed.reshape(images, across, across, WIN, WIN, channels).transpose(0, 1, 3, 2, 4, 5)
    image_grid = image_grid.reshape(images, GRID, GRID, channels)
    if shift_offset:
        image_grid = jnp.roll(image_grid, (shift_offset, shift_offset), axis=(1, 2))
    return image_grid.reshape(images * GRID * GRID, channels)

def window_allowed(region_ids, windows_count):
    across = GRID // WIN
    labels = region_ids.reshape(across, WIN, across, WIN).transpose(0, 2, 1, 3).reshape(across * across, WIN * WIN)
    agrees = labels[:, :, None] == labels[:, None, :]
    return jnp.tile(agrees, (windows_count // (across * across), 1, 1))[:, None]

def score_block(queries, key_bf, pairwise_bias, permitted_mask):
    scores = jnp.einsum('wqhd,wkhd->whqk', queries.astype(jnp.float32), key_bf.astype(jnp.float32)) + pairwise_bias[None]
    if permitted_mask is not None:
        scores = jnp.where(permitted_mask, scores, excluded_score)
    return scores

def attention_forward(qkv, pairwise_bias, permitted_mask, shift_offset, head_count):
    local_width = qkv.shape[1] // 3
    head_size = local_width // head_count
    windowed = to_windows(qkv, shift_offset)
    windows_count = windowed.shape[0]
    windowed = windowed.reshape(windows_count, WIN * WIN, 3, head_count, head_size)
    queries = to_bf16(windowed[:, :, 0] * head_size ** (-0.5))
    key_bf = to_bf16(windowed[:, :, 1])
    values = to_bf16(windowed[:, :, 2])
    scores = score_block(queries, key_bf, pairwise_bias, permitted_mask)
    highest = lax.optimization_barrier(jnp.max(scores, axis=-1, keepdims=True))
    log_total = highest + jnp.log(lax.optimization_barrier(jnp.sum(jnp.exp(scores - highest), axis=-1, keepdims=True)))
    probability = to_bf16(jnp.exp(scores - log_total))
    mixture = jnp.einsum('whqk,wkhd->wqhd', probability.astype(jnp.float32), values.astype(jnp.float32))
    attention_output = from_windows(to_bf16(mixture).reshape(windows_count, WIN * WIN, local_width), shift_offset)
    return (attention_output, (queries, key_bf, values, log_total))

def attention_backward(d_attended, stored_state, pairwise_bias, permitted_mask, shift_offset):
    queries, key_bf, values, log_total = stored_state
    windows_count, places, head_count, head_size = queries.shape
    d_mixture = to_windows(d_attended, shift_offset).reshape(windows_count, places, head_count, head_size).astype(jnp.float32)
    scores = score_block(queries, key_bf, pairwise_bias, permitted_mask)
    probability = jnp.exp(scores - log_total)
    prob_bf = to_bf16(probability).astype(jnp.float32)
    d_prob = jnp.einsum('wqhd,wkhd->whqk', d_mixture, values.astype(jnp.float32))
    d_values = jnp.einsum('whqk,wqhd->wkhd', prob_bf, d_mixture)
    d_scores = probability * (d_prob - lax.optimization_barrier(jnp.sum(probability * d_prob, axis=-1, keepdims=True)))
    d_bias = lax.optimization_barrier(jnp.sum(d_scores, axis=0))
    d_scores_bf = to_bf16(d_scores).astype(jnp.float32)
    d_queries = jnp.einsum('whqk,wkhd->wqhd', d_scores_bf, key_bf.astype(jnp.float32)) * head_size ** (-0.5)
    d_keys = jnp.einsum('whqk,wqhd->wkhd', d_scores_bf, queries.astype(jnp.float32))
    stacked = jnp.stack([d_queries, d_keys, d_values], axis=2).reshape(windows_count, places, 3 * head_count * head_size)
    return (from_windows(stacked, shift_offset), d_bias)

def block_pass(tokens, cot_block, qkv_weight, proj_weight, fc1_weight, fc2_weight, layer_norm_gains, layer_norm_biases, qv_bias, out_bias, fc1_bias, rel_table, rel_index, region_ids):
    residual_state = tokens.astype(jnp.float32)
    retained_layer_states = []
    for current_layer_index in range(LAYERS):
        shift_offset = SHIFT if current_layer_index % 2 == 1 else 0
        pairwise_bias = jnp.transpose(rel_table[current_layer_index][rel_index], (2, 0, 1))
        permitted_mask = window_allowed(region_ids, residual_state.shape[0] // (WIN * WIN)) if shift_offset else None
        normalized_rows, first_standardized, first_inverse_deviation = layer_norm_forward(residual_state, layer_norm_gains[current_layer_index, 0], layer_norm_biases[current_layer_index, 0])
        normalized_half_precision = to_bf16(normalized_rows)
        query_matrix = qkv_weight[current_layer_index].reshape(D, 3 * D)
        qkv_bias = jnp.concatenate([qv_bias[current_layer_index, 0], jnp.zeros((D,), jnp.float32), qv_bias[current_layer_index, 1]])
        qkv = jnp.dot(normalized_half_precision, query_matrix, preferred_element_type=jnp.float32) + qkv_bias
        attention_output, stored_state = attention_forward(qkv, pairwise_bias, permitted_mask, shift_offset, HEADS)
        middle_residual = residual_state + (jnp.dot(attention_output, proj_weight[current_layer_index], preferred_element_type=jnp.float32) + out_bias[current_layer_index, 0])
        second_normalized, second_standardized, second_inverse_deviation = layer_norm_forward(middle_residual, layer_norm_gains[current_layer_index, 1], layer_norm_biases[current_layer_index, 1])
        second_half_precision = to_bf16(second_normalized)
        preactivation_value = jnp.dot(second_half_precision, fc1_weight[current_layer_index], preferred_element_type=jnp.float32) + fc1_bias[current_layer_index]
        hidden_half_precision = to_bf16(gelu_value(preactivation_value))
        residual_state = middle_residual + (jnp.dot(hidden_half_precision, fc2_weight[current_layer_index], preferred_element_type=jnp.float32) + out_bias[current_layer_index, 1])
        retained_layer_states.append((shift_offset, pairwise_bias, permitted_mask, first_standardized, first_inverse_deviation, normalized_half_precision, query_matrix, stored_state, attention_output, second_standardized, second_inverse_deviation, second_half_precision, preactivation_value, hidden_half_precision))
    output = residual_state.astype(jnp.bfloat16)
    stream_grad = cot_block.astype(jnp.float32)
    results = [None] * LAYERS
    for current_layer_index in reversed(range(LAYERS)):
        shift_offset, pairwise_bias, permitted_mask, first_standardized, first_inverse_deviation, normalized_half_precision, query_matrix, stored_state, attention_output, second_standardized, second_inverse_deviation, second_half_precision, preactivation_value, hidden_half_precision = retained_layer_states[current_layer_index]
        d_out_mlp = lax.optimization_barrier(jnp.sum(stream_grad, axis=0))
        grad_bf = to_bf16(stream_grad)
        d_fc2 = jnp.dot(hidden_half_precision.T, grad_bf, preferred_element_type=jnp.float32)
        d_pre = jnp.dot(grad_bf, fc2_weight[current_layer_index].T, preferred_element_type=jnp.float32) * gelu_slope(preactivation_value)
        d_fc1_bias = lax.optimization_barrier(jnp.sum(d_pre, axis=0))
        d_pre_bf = to_bf16(d_pre)
        d_fc1 = jnp.dot(second_half_precision.T, d_pre_bf, preferred_element_type=jnp.float32)
        second_norm_gradient = jnp.dot(d_pre_bf, fc1_weight[current_layer_index].T, preferred_element_type=jnp.float32)
        middle_norm_gradient, second_gain_gradient, second_bias_gradient = layer_norm_backward(second_norm_gradient, second_standardized, second_inverse_deviation, layer_norm_gains[current_layer_index, 1])
        d_middle = stream_grad + middle_norm_gradient
        d_out_attn = lax.optimization_barrier(jnp.sum(d_middle, axis=0))
        middle_bf = to_bf16(d_middle)
        d_proj = jnp.dot(attention_output.T, middle_bf, preferred_element_type=jnp.float32)
        d_attended = to_bf16(jnp.dot(middle_bf, proj_weight[current_layer_index].T, preferred_element_type=jnp.float32))
        d_qkv, d_bias = attention_backward(d_attended, stored_state, pairwise_bias, permitted_mask, shift_offset)
        d_qv = jnp.stack([lax.optimization_barrier(jnp.sum(d_qkv[:, :D], axis=0)), lax.optimization_barrier(jnp.sum(d_qkv[:, 2 * D:], axis=0))])
        d_qkv_bf = to_bf16(d_qkv)
        d_qkv_weight = jnp.dot(normalized_half_precision.T, d_qkv_bf, preferred_element_type=jnp.float32).reshape(D, 3, D)
        normalized_gradient = jnp.dot(d_qkv_bf, query_matrix.T, preferred_element_type=jnp.float32)
        residual_norm_gradient, first_gain_gradient, first_bias_gradient = layer_norm_backward(normalized_gradient, first_standardized, first_inverse_deviation, layer_norm_gains[current_layer_index, 0])
        stream_grad = d_middle + residual_norm_gradient
        d_table = jnp.zeros((TABLE, HEADS), jnp.float32).at[rel_index.reshape(-1)].add(d_bias.reshape(HEADS, -1).T)
        results[current_layer_index] = (d_qkv_weight, d_proj, d_fc1, d_fc2, jnp.stack([first_gain_gradient, second_gain_gradient]), jnp.stack([first_bias_gradient, second_bias_gradient]), d_qv, jnp.stack([d_out_attn, d_out_mlp]), d_fc1_bias, d_table)
    grads = tuple((jnp.stack([results[index][member] for index in range(LAYERS)]) for member in range(10)))
    return (output, stream_grad, grads)

def reference(x_in, cot, qkv_weight, proj_weight, fc1_weight, fc2_weight, layer_norm_gains, layer_norm_biases, qv_bias, out_bias, fc1_bias, rel_table, rel_index, region_ids):
    block_rows = TOKENS // N_DP
    inputs = x_in.reshape(N_DP, block_rows, D)
    cotangents = cot.reshape(N_DP, block_rows, D)
    params = (qkv_weight, proj_weight, fc1_weight, fc2_weight, layer_norm_gains, layer_norm_biases, qv_bias, out_bias, fc1_bias, rel_table)
    initial = tuple((jnp.zeros(member.shape, jnp.float32) for member in params))

    def advance(carry, pair):
        output, stream_grad, grads = block_pass(pair[0], pair[1], qkv_weight, proj_weight, fc1_weight, fc2_weight, layer_norm_gains, layer_norm_biases, qv_bias, out_bias, fc1_bias, rel_table, rel_index, region_ids)
        return (tuple((total + grad_part for total, grad_part in zip(carry, grads))), (output, stream_grad))
    totals, (outputs, input_grads) = lax.scan(advance, initial, (inputs, cotangents))
    return (outputs.reshape(TOKENS, D), input_grads.reshape(TOKENS, D), totals[0], totals[1], totals[2], totals[3], totals[4], totals[5], totals[6], totals[7], totals[8], totals[9])
```

```python
import functools

import jax
import jax.numpy as jnp
from jax import lax
from jax.experimental import pallas as pl
from jax.experimental.pallas import tpu as pltpu
from jax.sharding import PartitionSpec as P

GRID = 14
WIN = 7
LAYERS = 2
HEAD_DIM = 32
SHIFT = 3
TABLE = 169
PLACES = WIN * WIN
CELLS = GRID * GRID
ROWS = 64
LANES = 4 * ROWS
CHUNK = 32

epsilon = 1e-05
excluded_score = -1e30
root_half = 0.7071067811865476
gauss_factor = 0.3989422804014327
head_scale = HEAD_DIM ** (-0.5)
bf16 = jnp.bfloat16
f32 = jnp.float32
VMEM_LIMIT = 60 * 1024 * 1024


def dot_nn(a, b):
    return lax.dot_general(a, b, (((1,), (0,)), ((), ())), preferred_element_type=f32)


def dot_nt(a, b):
    return lax.dot_general(a, b, (((1,), (1,)), ((), ())), preferred_element_type=f32)


def dot_tn(a, b):
    return lax.dot_general(a, b, (((0,), (0,)), ((), ())), preferred_element_type=f32)


def standardize(rows):
    centered = rows - jnp.mean(rows, axis=-1, keepdims=True)
    inverse = lax.rsqrt(jnp.mean(centered * centered, axis=-1, keepdims=True) + epsilon)
    return centered * inverse, inverse


def norm_backward(gradient, standard, inverse, gain):
    scaled = gradient * gain
    return inverse * (
        scaled
        - jnp.mean(scaled, axis=-1, keepdims=True)
        - standard * jnp.mean(scaled * standard, axis=-1, keepdims=True)
    )


def fold_rows(values):
    rows, columns = values.shape
    return jnp.sum(values.reshape(rows // 8, 8, columns), axis=0)


def weight_copy(place, owners, piece, index, column, matrix, sem):
    owner = owners[place]
    row = pl.multiple_of((owner >> 1) * CHUNK, CHUNK)
    return pltpu.make_async_copy(
        piece.at[index, :, pl.ds(column, matrix.shape[2])], matrix.at[owner & 1, pl.ds(row, CHUNK), :], sem
    )


def load_matrix(owners, pieces, column, matrix, sem):
    place = 0
    copies = []
    for piece in pieces:
        for index in range(piece.shape[0]):
            copies.append(weight_copy(place, owners, piece, index, column, matrix, sem))
            place += 1
    for copy in copies:
        copy.start()
    return copies


def store_matrix(owners, matrix, kept, sent, column, sem):
    copies = []
    half = kept.shape[0]
    for place in range(2 * half):
        owner = owners[place]
        row = pl.multiple_of((owner >> 1) * CHUNK, CHUNK)
        blocks = kept if place < half else sent
        copies.append(
            pltpu.make_async_copy(
                matrix.at[owner & 1, pl.ds(row, CHUNK), :],
                blocks.at[place % half, :, pl.ds(column, matrix.shape[2])],
                sem,
            )
        )
    for copy in copies:
        copy.start()
    for copy in copies:
        copy.wait()


def expand_heads(block, head_mask):
    return jnp.concatenate([block] * 4, axis=0) * head_mask


def gather_heads(stack):
    lane = lax.broadcasted_iota(jnp.int32, (ROWS, 128), 1)
    parts = [stack[h * ROWS : (h + 1) * ROWS] for h in range(4)]
    return jnp.where(
        lane < 64,
        jnp.where(lane < 32, parts[0], parts[1]),
        jnp.where(lane < 96, parts[2], parts[3]),
    )


def attention_forward_kernel(masked, count, owners_ref, *refs):
    pieces = refs[:count]
    (
        x_ref, norm_ref, qkv_bias_ref, out_bias_ref, bias_ref, mask_ref, head_mask_ref,
        to_windows_ref, from_windows_ref,
        middle_ref, qkv_ref, prob_ref, attended_ref,
        matrix, sem,
    ) = refs[count:]

    @pl.when(pl.program_id(0) == 0)
    def _():
        for copy in load_matrix(owners_ref, pieces, 0, matrix, sem):
            copy.wait()

    standard, _ = standardize(x_ref[...])
    normed = (standard * norm_ref[0:1] + norm_ref[1:2]).astype(bf16)
    windowed = dot_nn(to_windows_ref[...], normed).astype(bf16)
    for side in range(2):
        qkv = dot_nn(windowed, matrix[side, :, 0:768]) + qkv_bias_ref[side]
        qkv_ref[side, :, 0:256] = (qkv[:, 0:256] * head_scale).astype(bf16)
        qkv_ref[side, :, 256:768] = qkv[:, 256:768].astype(bf16)

    def one_window(window, carry):
        rows = pl.ds(pl.multiple_of(window * ROWS, ROWS), ROWS)
        for group in range(4):
            side, first = group // 2, (group % 2) * 128
            queries = expand_heads(qkv_ref[side, rows, first : first + 128], head_mask_ref[...])
            keys = qkv_ref[side, rows, 256 + first : 384 + first]
            values = qkv_ref[side, rows, 512 + first : 640 + first]
            scores = dot_nt(keys, queries) + bias_ref[group]
            if masked:
                scores = scores + mask_ref[window & 3]
            weights = jnp.exp(scores - jnp.max(scores, axis=0, keepdims=True))
            prob = (weights * (1.0 / jnp.sum(weights, axis=0, keepdims=True))).astype(bf16)
            prob_ref[window * 4 + group] = prob
            mixture = gather_heads(dot_tn(prob, values))
            attended_ref[rows, group * 128 : group * 128 + 128] = mixture.astype(bf16)
        return carry

    lax.fori_loop(0, x_ref.shape[0] // PLACES, one_window, 0)
    attended = dot_nn(from_windows_ref[...], attended_ref[...]).astype(bf16)
    total = x_ref[...] + out_bias_ref[...]
    for side in range(2):
        total = total + dot_nt(attended[:, side * 256 : side * 256 + 256], matrix[side, :, 768:1024])
    middle_ref[...] = total


def attention_backward_kernel(count, owners_ref, *refs):
    pieces = refs[:count]
    (
        grad_ref, x_ref, norm_ref, head_mask_ref, to_windows_ref, from_windows_ref,
        qkv_ref, prob_ref, attended_ref,
        out_ref, kept_ref, sent_ref, sums_ref, qv_sums_ref, bias_grad_ref,
        matrix, gradient, rounded, d_attended, d_qkv, sem,
    ) = refs[count:]
    step = pl.program_id(0)

    @pl.when(step == 0)
    def _():
        copies = load_matrix(owners_ref, pieces, 0, matrix, sem)
        gradient[...] = jnp.zeros_like(gradient)
        sums_ref[...] = jnp.zeros_like(sums_ref)
        qv_sums_ref[...] = jnp.zeros_like(qv_sums_ref)
        bias_grad_ref[...] = jnp.zeros_like(bias_grad_ref)
        for copy in copies:
            copy.wait()

    middle = dot_nn(to_windows_ref[...], grad_ref[...].astype(bf16)).astype(bf16)
    for side in range(2):
        half = slice(side * 256, side * 256 + 256)
        gradient[side, :, 768:1024] += dot_tn(middle, attended_ref[:, half])
        d_attended[:, half] = dot_nn(middle, matrix[side, :, 768:1024]).astype(bf16)

    def one_window(window, carry):
        rows = pl.ds(pl.multiple_of(window * ROWS, ROWS), ROWS)
        for group in range(4):
            side, first = group // 2, (group % 2) * 128
            head_mask = head_mask_ref[...]
            queries = expand_heads(qkv_ref[side, rows, first : first + 128], head_mask)
            keys = qkv_ref[side, rows, 256 + first : 384 + first]
            values = qkv_ref[side, rows, 512 + first : 640 + first]
            mixed = expand_heads(d_attended[rows, group * 128 : group * 128 + 128], head_mask)
            prob_bf = prob_ref[window * 4 + group]
            prob = prob_bf.astype(f32)
            weighted = prob * dot_nt(values, mixed)
            d_scores = weighted - prob * jnp.sum(weighted, axis=0, keepdims=True)
            bias_grad_ref[group] += d_scores
            d_scores_bf = d_scores.astype(bf16)
            d_values = dot_nn(prob_bf, mixed)
            d_keys = dot_nn(d_scores_bf, queries)
            d_queries = gather_heads(dot_tn(d_scores_bf, keys)) * head_scale
            qv_sums_ref[0, :, group * 128 : group * 128 + 128] += fold_rows(d_queries)
            qv_sums_ref[1, :, group * 128 : group * 128 + 128] += fold_rows(d_values)
            d_qkv[side, rows, first : first + 128] = d_queries.astype(bf16)
            d_qkv[side, rows, 256 + first : 384 + first] = d_keys.astype(bf16)
            d_qkv[side, rows, 512 + first : 640 + first] = d_values.astype(bf16)
        return carry

    lax.fori_loop(0, x_ref.shape[0] // PLACES, one_window, 0)
    standard, inverse = standardize(x_ref[...])
    gain = norm_ref[0:1]
    normed = (standard * gain + norm_ref[1:2]).astype(bf16)
    windowed = dot_nn(to_windows_ref[...], normed).astype(bf16)
    d_windowed = None
    for side in range(2):
        gradient[side, :, 0:768] += dot_tn(windowed, d_qkv[side])
        part = dot_nt(d_qkv[side], matrix[side, :, 0:768])
        d_windowed = part if d_windowed is None else d_windowed + part
    d_normed = dot_nn(from_windows_ref[...], d_windowed.astype(bf16))
    sums_ref[0] += fold_rows(d_normed * standard)
    sums_ref[1] += fold_rows(d_normed)
    out_ref[...] = grad_ref[...] + norm_backward(d_normed, standard, inverse, gain)

    @pl.when(step == pl.num_programs(0) - 1)
    def _():
        rounded[...] = gradient[...].astype(bf16)
        store_matrix(owners_ref, rounded, kept_ref, sent_ref, 0, sem)


def mlp_forward_kernel(count, owners_ref, *refs):
    pieces = refs[:count]
    (
        middle_ref, norm_ref, hidden_bias_ref, out_bias_ref,
        stream_ref, hidden_ref, slope_ref,
        first_matrix, second_matrix, normed, sem,
    ) = refs[count:]
    step = pl.program_id(0)
    width = hidden_ref.shape[1]

    @pl.when(step == 0)
    def _():
        copies = load_matrix(owners_ref, pieces, 0, first_matrix, sem)
        copies += load_matrix(owners_ref, pieces, 1024, second_matrix, sem)
        standard, _ = standardize(middle_ref[...])
        normed[...] = (standard * norm_ref[0:1] + norm_ref[1:2]).astype(bf16)
        stream_ref[...] = middle_ref[...] + out_bias_ref[...]
        for copy in copies:
            copy.wait()

    per_side = 1024 // width
    side = step // per_side
    columns = pl.ds(pl.multiple_of((step % per_side) * width, width), width)
    pre = dot_nn(normed[...], first_matrix[side, :, columns]) + hidden_bias_ref[...]
    area = 0.5 * (1.0 + lax.erf(pre * root_half))
    hidden = (pre * area).astype(bf16)
    hidden_ref[...] = hidden
    slope_ref[...] = (area + pre * jnp.exp(-0.5 * pre * pre) * gauss_factor).astype(bf16)
    stream_ref[...] += dot_nt(hidden, second_matrix[side, :, columns])


def mlp_backward_kernel(fused, count, owners_ref, *refs):
    pieces = refs[:count]
    refs = refs[count:]
    if fused:
        (
            grad_ref, middle_ref, norm_ref, hidden_bias_ref, out_bias_ref,
            stream_ref, d_middle_ref, kept_ref, sent_ref, sums_ref, bias_sums_ref,
            first_matrix, second_matrix, normed, normed_t, grad_bf, grad_t,
            first_gradient, second_gradient, total, stream, sem,
        ) = refs
    else:
        (
            grad_ref, middle_ref, norm_ref, hidden_ref, slope_ref,
            d_middle_ref, kept_ref, sent_ref, sums_ref, bias_sums_ref,
            first_matrix, second_matrix, normed, normed_t, grad_bf, grad_t,
            first_gradient, second_gradient, total, sem,
        ) = refs
    step = pl.program_id(0)
    width = bias_sums_ref.shape[1]

    @pl.when(step == 0)
    def _():
        copies = load_matrix(owners_ref, pieces, 0, first_matrix, sem)
        copies += load_matrix(owners_ref, pieces, 1024, second_matrix, sem)
        standard, _ = standardize(middle_ref[...])
        rows = (standard * norm_ref[0:1] + norm_ref[1:2]).astype(bf16)
        normed[...] = rows
        normed_t[...] = rows.T
        gradient = grad_ref[...].astype(bf16)
        grad_bf[...] = gradient
        grad_t[...] = gradient.T
        total[...] = jnp.zeros_like(total)
        if fused:
            stream[...] = middle_ref[...] + out_bias_ref[...]
        for copy in copies:
            copy.wait()

    per_side = 1024 // width
    side = step // per_side
    columns = pl.ds(pl.multiple_of((step % per_side) * width, width), width)
    if fused:
        pre = dot_nn(normed[...], first_matrix[side, :, columns]) + hidden_bias_ref[...]
        area = 0.5 * (1.0 + lax.erf(pre * root_half))
        hidden = (pre * area).astype(bf16)
        slope = area + pre * jnp.exp(-0.5 * pre * pre) * gauss_factor
        stream[...] += dot_nt(hidden, second_matrix[side, :, columns])
    else:
        hidden = hidden_ref[...]
        slope = slope_ref[...].astype(f32)
    d_pre = dot_nn(grad_bf[...], second_matrix[side, :, columns]) * slope
    bias_sums_ref[...] = fold_rows(d_pre)
    d_pre_bf = d_pre.astype(bf16)
    second_gradient[side, :, columns] = dot_nn(grad_t[...], hidden).astype(bf16)
    first_gradient[side, :, columns] = dot_nn(normed_t[...], d_pre_bf).astype(bf16)
    total[...] += dot_nt(d_pre_bf, first_matrix[side, :, columns])

    @pl.when(step == pl.num_programs(0) - 1)
    def _():
        d_second = total[...]
        gradient = grad_ref[...]
        standard, inverse = standardize(middle_ref[...])
        d_middle = gradient + norm_backward(d_second, standard, inverse, norm_ref[0:1])
        d_middle_ref[...] = d_middle
        sums_ref[0] = fold_rows(d_second * standard)
        sums_ref[1] = fold_rows(d_second)
        sums_ref[2] = fold_rows(d_middle)
        sums_ref[3] = fold_rows(gradient)
        if fused:
            stream_ref[...] = stream[...].astype(bf16)
        store_matrix(owners_ref, first_gradient, kept_ref, sent_ref, 0, sem)
        store_matrix(owners_ref, second_gradient, kept_ref, sent_ref, 1024, sem)


def params_of(steps=1):
    return pltpu.CompilerParams(
        dimension_semantics=("arbitrary",), vmem_limit_bytes=VMEM_LIMIT
    )


def whole_block(shape):
    return pl.BlockSpec(shape, lambda *_: (0,) * len(shape))


ANYWHERE = pl.BlockSpec(memory_space=pl.ANY)


def grid_spec(steps, in_specs, out_specs, scratch):
    return pltpu.PrefetchScalarGridSpec(
        num_scalar_prefetch=1, grid=(steps,), in_specs=in_specs, out_specs=out_specs,
        scratch_shapes=scratch,
    )


def attention_forward(own, pieces, x, norm, qkv_bias, out_bias, bias, mask, constants):
    head_mask, to_windows, from_windows = constants
    tokens, depth = x.shape
    pair = from_windows.shape[0]
    steps = tokens // pair
    windows = pair // PLACES
    masked = mask is not None
    if not masked:
        mask = jnp.zeros((1, 8, 128), f32)
    row_block = pl.BlockSpec((pair, depth), lambda i, *_: (i, 0))
    return pl.pallas_call(
        functools.partial(attention_forward_kernel, masked, len(pieces)),
        out_shape=(
            jax.ShapeDtypeStruct((tokens, depth), f32),
            jax.ShapeDtypeStruct((2, steps * windows * ROWS, 768), bf16),
            jax.ShapeDtypeStruct((steps * windows * 4, ROWS, LANES), bf16),
            jax.ShapeDtypeStruct((steps * windows * ROWS, depth), bf16),
        ),
        grid_spec=grid_spec(
            steps,
            [ANYWHERE] * len(pieces)
            + [row_block]
            + [whole_block(a.shape) for a in (norm, qkv_bias, out_bias, bias, mask, head_mask, to_windows, from_windows)],
            (
                row_block,
                pl.BlockSpec((2, windows * ROWS, 768), lambda i, *_: (0, i, 0)),
                pl.BlockSpec((windows * 4, ROWS, LANES), lambda i, *_: (i, 0, 0)),
                pl.BlockSpec((windows * ROWS, depth), lambda i, *_: (i, 0)),
            ),
            [pltpu.VMEM((2, depth, 1024), bf16), pltpu.SemaphoreType.DMA],
        ),
        compiler_params=params_of(),
        name="attention_forward",
    )(own, *pieces, x, norm, qkv_bias, out_bias, bias, mask, head_mask, to_windows, from_windows)


def attention_backward(own, pieces, grad, x, norm, saved, constants):
    head_mask, to_windows, from_windows = constants
    qkv, prob, attended = saved
    tokens, depth = x.shape
    pair = from_windows.shape[0]
    steps = tokens // pair
    windows = pair // PLACES
    row_block = pl.BlockSpec((pair, depth), lambda i, *_: (i, 0))
    blocks = depth // CHUNK
    return pl.pallas_call(
        functools.partial(attention_backward_kernel, len(pieces)),
        out_shape=(
            jax.ShapeDtypeStruct((tokens, depth), f32),
            jax.ShapeDtypeStruct((blocks, CHUNK, 1024), bf16),
            jax.ShapeDtypeStruct((blocks, CHUNK, 1024), bf16),
            jax.ShapeDtypeStruct((2, 8, depth), f32),
            jax.ShapeDtypeStruct((2, 8, depth), f32),
            jax.ShapeDtypeStruct((4, ROWS, LANES), f32),
        ),
        grid_spec=grid_spec(
            steps,
            [ANYWHERE] * len(pieces)
            + [row_block, row_block]
            + [whole_block(a.shape) for a in (norm, head_mask, to_windows, from_windows)]
            + [
                pl.BlockSpec((2, windows * ROWS, 768), lambda i, *_: (0, i, 0)),
                pl.BlockSpec((windows * 4, ROWS, LANES), lambda i, *_: (i, 0, 0)),
                pl.BlockSpec((windows * ROWS, depth), lambda i, *_: (i, 0)),
            ],
            (
                row_block,
                ANYWHERE,
                ANYWHERE,
                whole_block((2, 8, depth)),
                whole_block((2, 8, depth)),
                whole_block((4, ROWS, LANES)),
            ),
            [
                pltpu.VMEM((2, depth, 1024), bf16),
                pltpu.VMEM((2, depth, 1024), f32),
                pltpu.VMEM((2, depth, 1024), bf16),
                pltpu.VMEM((windows * ROWS, depth), bf16),
                pltpu.VMEM((2, windows * ROWS, 768), bf16),
                pltpu.SemaphoreType.DMA,
            ],
        ),
        compiler_params=params_of(),
        name="attention_backward",
    )(own, *pieces, grad, x, norm, head_mask, to_windows, from_windows, qkv, prob, attended)


FORWARD_WIDTH = 512
BACKWARD_WIDTH = 512


def mlp_forward(own, pieces, middle, norm, hidden_bias, out_bias):
    tokens, depth = middle.shape
    hidden_units = hidden_bias.shape[1]
    width = FORWARD_WIDTH
    column_block = pl.BlockSpec((tokens, width), lambda i, *_: (0, i))
    return pl.pallas_call(
        functools.partial(mlp_forward_kernel, len(pieces)),
        out_shape=(
            jax.ShapeDtypeStruct((tokens, depth), f32),
            jax.ShapeDtypeStruct((tokens, hidden_units), bf16),
            jax.ShapeDtypeStruct((tokens, hidden_units), bf16),
        ),
        grid_spec=grid_spec(
            hidden_units // width,
            [ANYWHERE] * len(pieces)
            + [
                whole_block(middle.shape),
                whole_block(norm.shape),
                pl.BlockSpec((1, width), lambda i, *_: (0, i)),
                whole_block(out_bias.shape),
            ],
            (whole_block(middle.shape), column_block, column_block),
            [
                pltpu.VMEM((2, depth, 1024), bf16),
                pltpu.VMEM((2, depth, 1024), bf16),
                pltpu.VMEM((tokens, depth), bf16),
                pltpu.SemaphoreType.DMA,
            ],
        ),
        compiler_params=params_of(),
        name="mlp_forward",
    )(own, *pieces, middle, norm, hidden_bias, out_bias)


def mlp_backward(own, pieces, grad, middle, norm, saved, hidden_bias, out_bias):
    tokens, depth = middle.shape
    hidden_units = hidden_bias.shape[1]
    width = BACKWARD_WIDTH
    fused = saved is None
    blocks = depth // CHUNK
    column_block = pl.BlockSpec((tokens, width), lambda i, *_: (0, i))
    full = whole_block(middle.shape)
    inputs = [grad, middle, norm]
    in_specs = [full, full, whole_block(norm.shape)]
    if fused:
        inputs += [hidden_bias, out_bias]
        in_specs += [pl.BlockSpec((1, width), lambda i, *_: (0, i)), whole_block(out_bias.shape)]
    else:
        inputs += list(saved)
        in_specs += [column_block, column_block]
    out_shape = [
        jax.ShapeDtypeStruct((tokens, depth), f32),
        jax.ShapeDtypeStruct((blocks, CHUNK, 2048), bf16),
        jax.ShapeDtypeStruct((blocks, CHUNK, 2048), bf16),
        jax.ShapeDtypeStruct((4, 8, depth), f32),
        jax.ShapeDtypeStruct((8, hidden_units), f32),
    ]
    out_specs = [
        full,
        ANYWHERE,
        ANYWHERE,
        whole_block((4, 8, depth)),
        pl.BlockSpec((8, width), lambda i, *_: (0, i)),
    ]
    scratch = [
        pltpu.VMEM((2, depth, 1024), bf16),
        pltpu.VMEM((2, depth, 1024), bf16),
        pltpu.VMEM((tokens, depth), bf16),
        pltpu.VMEM((depth, tokens), bf16),
        pltpu.VMEM((tokens, depth), bf16),
        pltpu.VMEM((depth, tokens), bf16),
        pltpu.VMEM((2, depth, 1024), bf16),
        pltpu.VMEM((2, depth, 1024), bf16),
        pltpu.VMEM((tokens, depth), f32),
    ]
    if fused:
        out_shape = [jax.ShapeDtypeStruct((tokens, depth), bf16)] + out_shape
        out_specs = [full] + out_specs
        scratch += [pltpu.VMEM((tokens, depth), f32)]
    return pl.pallas_call(
        functools.partial(mlp_backward_kernel, fused, len(pieces)),
        out_shape=tuple(out_shape),
        grid_spec=grid_spec(
            hidden_units // width,
            [ANYWHERE] * len(pieces) + in_specs,
            tuple(out_specs),
            scratch + [pltpu.SemaphoreType.DMA],
        ),
        compiler_params=params_of(),
        name="mlp_fused" if fused else "mlp_backward",
    )(own, *pieces, *inputs)


def window_order(shift, images):
    across = GRID // WIN
    row = jnp.arange(images * across * across * ROWS, dtype=jnp.int32)
    place = row % ROWS
    window = row // ROWS % (across * across)
    image = row // (ROWS * across * across)
    down = (window // across * WIN + place // WIN + shift) % GRID
    right = (window % across * WIN + place % WIN + shift) % GRID
    token = jnp.where(place < PLACES, image * CELLS + down * GRID + right, -1)
    return (token[:, None] == jnp.arange(images * CELLS, dtype=jnp.int32)[None, :]).astype(bf16)


def padded_index(rel_index):
    pad = ROWS - PLACES
    return jnp.pad(rel_index.T, ((0, pad), (0, pad)), constant_values=-1)


def pair_bias(selector, table):
    heads = table.shape[1]
    flat = jnp.dot(table.T, selector, precision=lax.Precision.HIGHEST)
    flat = flat.reshape(heads // 4, 4, ROWS, ROWS).transpose(0, 2, 1, 3).reshape(heads // 4, ROWS, LANES)
    is_key = jnp.arange(ROWS)[None, :, None] < PLACES
    return jnp.where(is_key, flat, excluded_score)


def window_mask(region_ids):
    across = GRID // WIN
    labels = (
        region_ids.reshape(across, WIN, across, WIN)
        .transpose(0, 2, 1, 3)
        .reshape(across * across, PLACES)
    )
    pad = ROWS - PLACES
    labels = jnp.pad(labels, ((0, 0), (0, pad)), constant_values=-1)
    agrees = labels[:, :, None] == labels[:, None, :]
    queries_only = jnp.arange(ROWS) >= PLACES
    agrees = agrees | queries_only[None, None, :]
    mask = jnp.where(agrees, 0.0, excluded_score).astype(f32)
    return jnp.tile(mask, (1, 1, 4))


X_BIT, CORE_BIT, Y_BIT, NEAR_BIT, FAR_BIT = 1, 2, 4, 8, 16


def exchange(block, even, odd):
    pairs = [(d, d ^ (odd if d & CORE_BIT else even)) for d in range(32)]
    return lax.ppermute(block, ("dp", "tensor"), pairs)


def local(
    x_in,
    cot,
    qkv_weight,
    proj_weight,
    fc1_weight,
    fc2_weight,
    layer_norm_gains,
    layer_norm_biases,
    qv_bias,
    out_bias,
    fc1_bias,
    rel_table,
    rel_index,
    region_ids,
):
    axes = ("dp", "tensor")
    depth = x_in.shape[1]
    parts = lax.axis_size("dp")
    owned_rows = depth // parts
    me = lax.axis_index("dp") * 2 + lax.axis_index("tensor")
    cube = parts == 16 and lax.axis_size("tensor") == 2 and owned_rows == CHUNK
    blocks_total = 2 * depth // CHUNK
    if cube:
        place = jnp.arange(blocks_total, dtype=jnp.int32)
        owner_core = ((me >> 1) & 1) ^ (place >> 4)
        third, fourth = (place >> 2) & 1, (place >> 3) & 1
        across = jnp.where(owner_core == 0, third * X_BIT + fourth * Y_BIT, third * Y_BIT + fourth * X_BIT)
        own = me ^ (((place & 1) * FAR_BIT) | (((place >> 1) & 1) * NEAR_BIT) | across | ((place >> 4) * CORE_BIT))
        own = own.astype(jnp.int32)
    else:
        own = jnp.arange(blocks_total, dtype=jnp.int32)

    def gather(block):
        columns = block.shape[1]
        if cube:
            held = block[None]
            for even, odd in ((FAR_BIT, FAR_BIT), (NEAR_BIT, NEAR_BIT), (X_BIT, Y_BIT)):
                held = jnp.concatenate([held, exchange(held, even, odd)], axis=0)
            other = exchange(held, Y_BIT, X_BIT)
            return (
                held, other, exchange(held, CORE_BIT, CORE_BIT), exchange(other, CORE_BIT, CORE_BIT)
            )
        rows = lax.all_gather(block, axes, axis=0, tiled=False)
        rows = rows.reshape(parts, 2, owned_rows, columns).transpose(1, 0, 2, 3)
        rows = rows.reshape(2, depth // CHUNK, CHUNK, columns).transpose(1, 0, 2, 3)
        return (rows.reshape(blocks_total, CHUNK, columns),)

    def scatter(kept, sent):
        if cube:
            for even, odd in (
                (CORE_BIT, CORE_BIT), (Y_BIT, X_BIT), (X_BIT, Y_BIT), (NEAR_BIT, NEAR_BIT), (FAR_BIT, FAR_BIT)
            ):
                received = exchange(sent, even, odd)
                half = kept.shape[0] // 2
                if half:
                    sent = kept[half:] + received[half:]
                    kept = kept[:half] + received[:half]
                else:
                    return kept[0].astype(f32) + received[0].astype(f32)
        columns = kept.shape[2]
        blocks = jnp.concatenate([kept, sent], axis=0)
        blocks = blocks.reshape(depth // CHUNK, 2, CHUNK, columns).transpose(1, 0, 2, 3)
        blocks = blocks.reshape(2, parts, owned_rows, columns).transpose(1, 0, 2, 3)
        blocks = blocks.reshape(2 * parts * owned_rows, columns)
        return lax.psum_scatter(blocks, axes, scatter_dimension=0, tiled=True).astype(f32)

    def total_of(vector):
        if cube:
            for bit in (CORE_BIT, X_BIT, Y_BIT, NEAR_BIT, FAR_BIT):
                vector = vector + exchange(vector, bit, bit)
            return vector
        return lax.psum(vector, axes)

    attention_weights, mlp_weights = [], []
    for layer in range(LAYERS):
        attention_weights.append(
            gather(
                jnp.concatenate(
                    [qkv_weight[layer].reshape(owned_rows, -1), proj_weight[layer].T], axis=1
                )
            )
        )
        mlp_weights.append(
            gather(jnp.concatenate([fc1_weight[layer], fc2_weight[layer].T], axis=1))
        )

    shared = jnp.concatenate([qv_bias.reshape(-1), fc1_bias.reshape(-1), rel_table.reshape(-1)])
    if cube:
        other = exchange(shared, X_BIT, X_BIT)
        first = lax.axis_index("tensor") == 0
        both = jnp.stack([jnp.where(first, shared, other), jnp.where(first, other, shared)])
    else:
        both = lax.all_gather(shared, "tensor", axis=0)
    all_qv_bias = both[:, : qv_bias.size].reshape((2,) + qv_bias.shape)
    all_fc1_bias = (
        both[:, qv_bias.size : qv_bias.size + fc1_bias.size]
        .reshape((2,) + fc1_bias.shape)
        .transpose(1, 0, 2)
        .reshape(LAYERS, -1)
    )
    all_table = (
        both[:, qv_bias.size + fc1_bias.size :]
        .reshape((2,) + rel_table.shape)
        .transpose(1, 2, 0, 3)
        .reshape(LAYERS, TABLE, -1)
    )
    selector = (
        padded_index(rel_index).reshape(1, -1) == jnp.arange(TABLE, dtype=jnp.int32)[:, None]
    ).astype(f32)
    lane = jnp.arange(128)[None, :] // HEAD_DIM
    head_mask = (lane == jnp.arange(LANES)[:, None] // ROWS).astype(bf16)
    constants = []
    for layer in range(LAYERS):
        order = window_order(SHIFT if layer % 2 else 0, 2)
        constants.append((head_mask, order, order.T))
    mask = window_mask(region_ids)

    def norm_rows(layer, which):
        return jnp.stack([layer_norm_gains[layer, which], layer_norm_biases[layer, which]])

    stream = x_in.astype(f32)
    streams, middles, saved_attention, saved_mlp = [], [], [], []
    for layer in range(LAYERS):
        streams.append(stream)
        query_bias = all_qv_bias[:, layer, 0]
        qkv_bias = jnp.concatenate(
            [query_bias, jnp.zeros_like(query_bias), all_qv_bias[:, layer, 1]], axis=1
        )[:, None, :]
        middle, qkv, prob, attended = attention_forward(
            own,
            attention_weights[layer],
            stream,
            norm_rows(layer, 0),
            qkv_bias,
            out_bias[layer, 0][None],
            pair_bias(selector, all_table[layer]),
            mask if layer % 2 else None,
            constants[layer],
        )
        saved_attention.append((qkv, prob, attended))
        middles.append(middle)
        if layer < LAYERS - 1:
            stream, hidden, slope = mlp_forward(
                own, mlp_weights[layer], middle,
                norm_rows(layer, 1), all_fc1_bias[layer][None], out_bias[layer, 1][None],
            )
            saved_mlp.append((hidden, slope))
        else:
            saved_mlp.append(None)

    grad = cot.astype(f32)
    results = [None] * LAYERS
    for layer in reversed(range(LAYERS)):
        outs = mlp_backward(
            own, mlp_weights[layer], grad, middles[layer],
            norm_rows(layer, 1), saved_mlp[layer], all_fc1_bias[layer][None],
            out_bias[layer, 1][None],
        )
        if saved_mlp[layer] is None:
            output, outs = outs[0], outs[1:]
        d_middle, kept, sent, mlp_sums, hidden_sums = outs
        owned_mlp = scatter(kept, sent)
        grad, kept, sent, attention_sums, qv_sums, bias_grad = attention_backward(
            own, attention_weights[layer], d_middle, streams[layer], norm_rows(layer, 0),
            saved_attention[layer], constants[layer],
        )
        owned_attention = scatter(kept, sent)
        heads = 4 * bias_grad.shape[0]
        d_bias = bias_grad.reshape(heads // 4, ROWS, 4, ROWS).transpose(0, 2, 1, 3)
        d_table = lax.dot_general(
            selector, d_bias.reshape(heads, -1), (((1,), (1,)), ((), ())),
            precision=lax.Precision.HIGHEST,
        )
        mlp_sums = jnp.sum(mlp_sums, axis=1)
        attention_sums = jnp.sum(attention_sums, axis=1)
        small = jnp.concatenate(
            [
                attention_sums[0], mlp_sums[0],
                attention_sums[1], mlp_sums[1],
                mlp_sums[2], mlp_sums[3],
                jnp.sum(qv_sums, axis=1).reshape(-1),
                jnp.sum(hidden_sums, axis=0),
                d_table.reshape(-1),
            ]
        )
        results[layer] = (owned_attention, owned_mlp, total_of(small))

    totals = jnp.stack([results[layer][2] for layer in range(LAYERS)])
    hidden_units = all_fc1_bias.shape[1]
    norm_gain = totals[:, : 2 * depth].reshape(LAYERS, 2, depth)
    norm_shift = totals[:, 2 * depth : 4 * depth].reshape(LAYERS, 2, depth)
    g_out_bias = totals[:, 4 * depth : 6 * depth].reshape(LAYERS, 2, depth)
    g_qv = totals[:, 6 * depth : 8 * depth].reshape(LAYERS, 2, 2, depth // 2)
    g_fc1_bias = totals[:, 8 * depth : 8 * depth + hidden_units].reshape(LAYERS, 2, -1)
    g_table = totals[:, 8 * depth + hidden_units :].reshape(LAYERS, TABLE, 2, -1)
    side = lax.axis_index("tensor")

    def mine(array, axis):
        return lax.dynamic_index_in_dim(array, side, axis, keepdims=False)

    attention_grads = jnp.stack([results[layer][0] for layer in range(LAYERS)])
    mlp_grads = jnp.stack([results[layer][1] for layer in range(LAYERS)])
    return (
        output,
        grad,
        attention_grads[:, :, :768].reshape(LAYERS, owned_rows, 3, -1),
        attention_grads[:, :, 768:].transpose(0, 2, 1),
        mlp_grads[:, :, :1024],
        mlp_grads[:, :, 1024:].transpose(0, 2, 1),
        norm_gain,
        norm_shift,
        mine(g_qv, 2),
        g_out_bias,
        mine(g_fc1_bias, 1),
        mine(g_table, 2),
    )


def solution(mesh):
    return jax.shard_map(
        local,
        mesh=mesh,
        in_specs=(
            P(("dp", "tensor"), None),
            P(("dp", "tensor"), None),
            P(None, "dp", None, "tensor"),
            P(None, "tensor", "dp"),
            P(None, "dp", "tensor"),
            P(None, "tensor", "dp"),
            P(),
            P(),
            P(None, None, "tensor"),
            P(),
            P(None, "tensor"),
            P(None, None, "tensor"),
            P(),
            P(),
        ),
        out_specs=(
            P(("dp", "tensor"), None),
            P(("dp", "tensor"), None),
            P(None, "dp", None, "tensor"),
            P(None, "tensor", "dp"),
            P(None, "dp", "tensor"),
            P(None, "tensor", "dp"),
            P(),
            P(),
            P(None, None, "tensor"),
            P(),
            P(None, "tensor"),
            P(None, None, "tensor"),
        ),
        check_vma=False,
    )
```
